32 devices in a mesh: tile: 16 (over z, y, x), spec: 2 (over core).
Axes of the slice: x: 2, y: 2, z: 4, core: 2. Of those that a mesh axis runs over, the one named last changes fastest.
Arguments:
- tracers: float32 [48, 2, 2048, 128], P('spec', None, 'tile'), may hold values from 0.1 to 10
- courant: float32 [2, 2, 2, 2, 2048, 128], P('spec', None, None, None, 'tile'), may hold values from -0.4 to 0.4
- diffusivity: float32 [2, 2, 2, 2, 2048, 128], P('spec', None, None, None, 'tile'), may hold values from 0.005 to 0.08
- edge_blocks: int32 [16, 4], P('tile'), may hold values from 0 to 15, as said below
- edge_flips: int32 [16, 4], P('tile'), may hold values from 0 to 1, as said below
- roots: int32 [2, 16], P(None, 'tile'), may hold values from 0 to 1
Outputs:
- transported: float32 [48, 2, 2048, 128], P('spec', None, 'tile')
The draws below stay inside these ranges and needn't reach their ends.
Inputs may be any that keep to these rules, and one draw needn't show every extreme that they name: `edge_blocks`: entries 0 to 3 of a row are the blocks across the west, east, south and north edges; if a is across b's east (north) edge then b is across a's west (south) edge; no block is across its own edge and the four blocks of a row differ. `edge_flips`: the flag of an edge equals the flag of the same edge seen from the block across it.
All inputs are finite; a program needn't handle non-finite values.
Results may differ from the reference program's by a relative error of at most 0.0003.
Values sent between devices are 32-bit elements; how exact they have to be, the bound alone decides.
A program may use at most 64 MiB of HBM per device.

```python
import math
import jax
import jax.numpy as jnp
from jax import lax

SPECIES = 48
LEV = 2
CELLS = 128
SUBSTEPS = 2
BLOCKS = 16
N_SPEC = 2


def torus_links(key):
    side_len = math.isqrt(BLOCKS)
    ordering = jax.random.permutation(jax.random.fold_in(key, 11), BLOCKS).astype(jnp.int32)
    position = jnp.argsort(ordering, stable=True).astype(jnp.int32)
    row_at = position // side_len
    col_at = position % side_len
    west_pos = row_at * side_len + (col_at - 1) % side_len
    east_pos = row_at * side_len + (col_at + 1) % side_len
    south_pos = (row_at - 1) % side_len * side_len + col_at
    north_pos = (row_at + 1) % side_len * side_len + col_at
    linked = jnp.stack([ordering[west_pos], ordering[east_pos], ordering[south_pos], ordering[north_pos]], 1).astype(jnp.int32)
    across = jax.random.randint(jax.random.fold_in(key, 23), (BLOCKS,), 0, 2, dtype=jnp.int32)
    upward = jax.random.randint(jax.random.fold_in(key, 29), (BLOCKS,), 0, 2, dtype=jnp.int32)
    turned = jnp.stack([across[west_pos], across[position], upward[south_pos], upward[position]], 1).astype(jnp.int32)
    return (linked, turned)


def draw_edge_blocks(key, part):
    return torus_links(key)[0]


def draw_edge_flips(key, part):
    return torus_links(key)[1]


def touch_ends(result, stream_key, low, top_value):
    index_at = [jax.random.randint(jax.random.fold_in(stream_key, axis), (), 0, length) for axis, length in enumerate(result.shape)]
    longest = result.shape.index(max(result.shape))
    beside = index_at[:longest] + [(index_at[longest] + 1) % result.shape[longest]] + index_at[longest + 1:]
    return result.at[tuple(index_at)].set(low).at[tuple(beside)].set(top_value)


def steps_of(key, extent, split, smallest, top_value):
    gain, own = 1.0, jax.random.fold_in(key, 6)
    for dim, parts in split:
        heights = jnp.exp(jax.random.uniform(jax.random.fold_in(own, dim), (parts,), jnp.float32, smallest / len(split), top_value / len(split)))
        gain = gain * jnp.repeat(heights, extent[dim] // parts).reshape([-1 if axis == dim else 1 for axis in range(len(extent))])
    return gain


def setup_inputs(seed: int = 0) -> dict:
    seeds = jax.random.split(jax.random.key(seed), 7)
    tracers = jnp.clip(jnp.exp(math.log(10.0) - 4.6051702 * jax.random.uniform(seeds[0], (SPECIES, LEV, BLOCKS * CELLS, CELLS), jnp.float32) ** steps_of(seeds[0], (SPECIES, LEV, BLOCKS * CELLS, CELLS), ((0, 2), (2, 16)), -0.2, 0.2)), 0.1, 10.0)
    courant = jnp.clip(jax.random.uniform(seeds[1], (N_SPEC, SUBSTEPS, 2, LEV, BLOCKS * CELLS, CELLS), jnp.float32, -0.4, 0.4) * steps_of(seeds[1], (N_SPEC, SUBSTEPS, 2, LEV, BLOCKS * CELLS, CELLS), ((0, 2), (4, 16)), -0.4, 0.0), -0.4, 0.4)
    diffusivity = jnp.clip(jnp.exp(math.log(0.08) - 2.7725887 * jax.random.uniform(seeds[2], (N_SPEC, SUBSTEPS, 2, LEV, BLOCKS * CELLS, CELLS), jnp.float32) ** steps_of(seeds[2], (N_SPEC, SUBSTEPS, 2, LEV, BLOCKS * CELLS, CELLS), ((0, 2), (4, 16)), -0.2, 0.2)), 0.005, 0.08)
    edge_blocks = draw_edge_blocks(jax.random.fold_in(seeds[6], 71), 0)
    edge_flips = draw_edge_flips(jax.random.fold_in(seeds[6], 71), 0)
    roots = touch_ends(jax.random.randint(seeds[5], (SUBSTEPS, BLOCKS), 0, N_SPEC), jax.random.fold_in(seeds[5], 1), 0, N_SPEC - 1).astype(jnp.int32)
    return {"tracers": tracers, "courant": courant, "diffusivity": diffusivity, "edge_blocks": edge_blocks, "edge_flips": edge_flips, "roots": roots}


def face_flux(padded, speed, kappa, along):
    inner = padded.shape[along] - 6

    def take_part(array, begin_at, end_at):
        return lax.slice_in_dim(array, begin_at, end_at, axis=along)

    edge_vals = (7.0 / 12.0) * (take_part(padded, 1, inner + 4) + take_part(padded, 2, inner + 5)) - (1.0 / 12.0) * (take_part(padded, 0, inner + 3) + take_part(padded, 3, inner + 6))
    lower_face = take_part(edge_vals, 0, inner + 1)
    centre = take_part(edge_vals, 1, inner + 2)
    upper_face = take_part(edge_vals, 2, inner + 3)
    behind = take_part(padded, 2, inner + 3)
    ahead_cell = take_part(padded, 3, inner + 4)
    reverse = -speed
    shape_pos = 6.0 * behind - 3.0 * (lower_face + centre)
    from_behind = centre - 0.5 * speed * ((centre - lower_face) - (1.0 - (2.0 / 3.0) * speed) * shape_pos)
    shape_neg = 6.0 * ahead_cell - 3.0 * (centre + upper_face)
    from_ahead = centre + 0.5 * reverse * ((upper_face - centre) + (1.0 - (2.0 / 3.0) * reverse) * shape_neg)
    face_val = jnp.where(speed > 0.0, from_behind, from_ahead)
    return speed * face_val - kappa * (ahead_cell - behind)


def edge_strips(field):
    west_side = jnp.swapaxes(field[..., :, 0:3], -1, -2)
    east_side = jnp.swapaxes(field[..., :, ::-1][..., :, 0:3], -1, -2)
    south_side = field[..., 0:3, :]
    north_side = field[..., ::-1, :][..., 0:3, :]
    return jnp.stack([west_side, east_side, south_side, north_side], 0)


def orient(strip_in, flipped):
    return jnp.where(flipped == 1, strip_in[..., ::-1], strip_in)


def advance(field, speed_x, speed_y, kappa_x, kappa_y, from_west, from_east, from_south, from_north, east_speed, east_kappa, north_speed, north_kappa):
    padded_x = jnp.concatenate([jnp.swapaxes(from_west[..., ::-1, :], -1, -2), field, jnp.swapaxes(from_east, -1, -2)], -1)
    padded_y = jnp.concatenate([from_south[..., ::-1, :], field, from_north], -2)
    faces_cx = jnp.concatenate([speed_x, east_speed[..., None]], -1)
    faces_kx = jnp.concatenate([kappa_x, east_kappa[..., None]], -1)
    faces_cy = jnp.concatenate([speed_y, north_speed[..., None, :]], -2)
    faces_ky = jnp.concatenate([kappa_y, north_kappa[..., None, :]], -2)
    flux_x = face_flux(padded_x, faces_cx, faces_kx, padded_x.ndim - 1)
    flux_y = face_flux(padded_y, faces_cy, faces_ky, padded_y.ndim - 2)
    return field - (flux_x[..., 1:] - flux_x[..., :-1]) - (flux_y[..., 1:, :] - flux_y[..., :-1, :])


def substep_all(field, speeds, kappas, neighbours, flips):
    strips = edge_strips(field)

    def fetch(source, edge):
        got = jnp.take(strips[source], neighbours[:, edge], axis=1)
        return orient(got, flips[:, edge][None, :, None, None])

    def face_fetch(values, edge):
        got = jnp.take(values, neighbours[:, edge], axis=1)
        return orient(got, flips[:, edge][None, :, None])

    east_speed = face_fetch(speeds[0][..., :, 0], 1)
    east_kappa = face_fetch(kappas[0][..., :, 0], 1)
    north_speed = face_fetch(speeds[1][..., 0, :], 3)
    north_kappa = face_fetch(kappas[1][..., 0, :], 3)
    return advance(field, speeds[0], speeds[1], kappas[0], kappas[1], fetch(1, 0), fetch(0, 1), fetch(3, 2), fetch(2, 3), east_speed, east_kappa, north_speed, north_kappa)


def pick_member(source, chosen):
    members = source.reshape(source.shape[0], 2, LEV, BLOCKS, CELLS, CELLS)
    index = chosen.astype(jnp.int32)[None, None, None, :, None, None]
    index = jnp.broadcast_to(index, (1, 2, LEV, BLOCKS, CELLS, CELLS))
    return jnp.take_along_axis(members, index, axis=0)[0]


def reference(tracers, courant, diffusivity, edge_blocks, edge_flips, roots):
    blocks_all = tracers.reshape(SPECIES, LEV, BLOCKS, CELLS, CELLS)
    fields = []
    for substep in range(SUBSTEPS):
        speeds = pick_member(courant[:, substep], roots[substep])
        kappas = pick_member(diffusivity[:, substep], roots[substep])
        fields.append((speeds, kappas))

    def one_species(field):
        for speeds, kappas in fields:
            field = substep_all(field, speeds, kappas, edge_blocks, edge_flips)
        return field

    moved = lax.map(one_species, blocks_all)
    return moved.reshape(SPECIES, LEV, BLOCKS * CELLS, CELLS)
```

```python
import functools

import jax
import jax.numpy as jnp
from jax import lax
from jax.experimental import pallas as pl
from jax.experimental.pallas import tpu as pltpu
from jax.sharding import PartitionSpec as P

MESH = pl.DeviceIdType.MESH
C = 128
PAD = 144
VMEM_LIMIT = 56 * 1024 * 1024


def greet_all(sizes, axis):
    n = sizes[axis]
    me = lax.axis_index(axis)
    barrier = pltpu.get_barrier_semaphore()

    @pl.loop(1, n)
    def _(off):
        pl.semaphore_signal(
            barrier, inc=1, device_id={axis: lax.rem(me + off, n)}, device_id_type=MESH
        )

    pl.semaphore_wait(barrier, n - 1)


def spread_kernel(sizes, cour, diff, cour_all, diff_all, send_sem, recv_sem, own_sem):
    n = sizes["spec"]
    me = lax.axis_index("spec")
    greet_all(sizes, "spec")
    own = [
        pltpu.make_async_copy(cour.at[0], cour_all.at[me], own_sem.at[0]),
        pltpu.make_async_copy(diff.at[0], diff_all.at[me], own_sem.at[1]),
    ]

    def copies(off):
        peer = lax.rem(me + off, n)
        return [
            pltpu.make_async_remote_copy(
                src_ref=src.at[0],
                dst_ref=dst.at[me],
                send_sem=send_sem.at[which, off],
                recv_sem=recv_sem.at[which, off],
                device_id={"spec": peer},
                device_id_type=MESH,
            )
            for which, (src, dst) in enumerate([(cour, cour_all), (diff, diff_all)])
        ]

    @pl.loop(1, n)
    def _(off):
        for copy in copies(off):
            copy.start()

    for copy in own:
        copy.start()
    for copy in own:
        copy.wait()

    @pl.loop(1, n)
    def _(off):
        for copy in copies(off):
            copy.wait()


def swap_kernel(sizes, slots, got, send_sem, recv_sem):
    n = sizes["tile"]
    me = lax.axis_index("tile")
    greet_all(sizes, "tile")

    def copy_to(off):
        peer = lax.rem(me + off, n)
        return pltpu.make_async_remote_copy(
            src_ref=slots.at[peer],
            dst_ref=got.at[me],
            send_sem=send_sem.at[off],
            recv_sem=recv_sem.at[off],
            device_id={"tile": peer},
            device_id_type=MESH,
        )

    @pl.loop(1, n)
    def _(off):
        copy_to(off).start()

    @pl.loop(1, n)
    def _(off):
        copy_to(off).wait()


def spread_fields(sizes, cour, diff):
    n = sizes["spec"]
    shape = jax.ShapeDtypeStruct((n,) + cour.shape[1:], cour.dtype)
    anywhere = pl.BlockSpec(memory_space=pl.ANY)
    return pl.pallas_call(
        functools.partial(spread_kernel, sizes),
        out_shape=(shape, shape),
        in_specs=[anywhere] * 2,
        out_specs=(anywhere, anywhere),
        scratch_shapes=[
            pltpu.SemaphoreType.DMA((2, n)),
            pltpu.SemaphoreType.DMA((2, n)),
            pltpu.SemaphoreType.DMA((2,)),
        ],
        compiler_params=pltpu.CompilerParams(collective_id=0, has_side_effects=True),
        name="spread_fields",
    )(cour, diff)


def swap_slots(sizes, slots, which):
    n = sizes["tile"]
    anywhere = pl.BlockSpec(memory_space=pl.ANY)
    return pl.pallas_call(
        functools.partial(swap_kernel, sizes),
        out_shape=jax.ShapeDtypeStruct(slots.shape, slots.dtype),
        in_specs=[anywhere],
        out_specs=anywhere,
        scratch_shapes=[pltpu.SemaphoreType.DMA((n,)), pltpu.SemaphoreType.DMA((n,))],
        compiler_params=pltpu.CompilerParams(collective_id=1 + which, has_side_effects=True),
        name=f"swap_slots_{which}",
    )(slots)


def groups_of(planes):
    return -(-planes // 16)


def lanes(rows):
    return lax.broadcasted_iota(jnp.int32, (rows, C), 1)


def pack_strips(planes, q, strips, turned):
    lane_group = lanes(C) // 8
    for g in range(groups_of(planes)):
        packed = jnp.zeros((C, C), jnp.float32)
        for slot in range(min(16, planes - 16 * g)):
            plane = q[pl.ds((16 * g + slot) * C, C), :]
            packed = jnp.where(lane_group == slot, pltpu.roll(plane, 8 * slot + 3, 1), packed)
        turned[pl.ds(g * C, C), :] = packed.T
    for d in range(3):
        rows = pl.ds(d * planes, planes)
        strips[0, rows, :] = turned[pl.ds(3 + d, planes, stride=8), :]
        strips[1, rows, :] = turned[pl.ds(2 - d, planes, stride=8), :]
        strips[2, rows, :] = q[pl.ds(d, planes, stride=C), :]
        strips[3, rows, :] = q[pl.ds(C - 1 - d, planes, stride=C), :]


def fill_slots(n, near, strips, slots):
    @pl.loop(0, n)
    def _(dest):
        edge = jnp.int32(0)
        for e in range(1, 4):
            edge = jnp.where(near[0, e] == dest, e, edge)
        slots[dest] = strips[edge]


def pack_kernel(sizes, planes, roots, near, q, cour0, cour1, diff0, diff1, slots, strips, turned):
    pack_strips(planes, q, strips, turned)
    lane = lanes(C)
    faces = jnp.zeros((C, C), jnp.float32)
    for k, fields in enumerate([(cour0, diff0), (cour1, diff1)]):
        for t, field in enumerate(fields):
            for lev in range(2):
                j = (k * 2 + t) * 2 + lev
                west = field[0, 0, 0, lev]
                west = pltpu.roll(west, j, 1) if j else west
                faces = jnp.where(lane == j, west, faces)
                strips[2, pl.ds(3 * planes + j, 1), :] = field[0, 0, 1, lev, 0:1, :]
    strips[0, pl.ds(3 * planes, 8), :] = faces.T[0:8]
    strips[1, pl.ds(3 * planes, 8), :] = jnp.zeros((8, C), jnp.float32)
    strips[3, pl.ds(3 * planes, 8), :] = jnp.zeros((8, C), jnp.float32)
    fill_slots(sizes["tile"], near, strips, slots)


def field_spec(k):
    return pl.BlockSpec(
        (1, 1, 2, 2, C, C), lambda i, roots, *_: (roots[k, 0], k, 0, 0, 0, 0)
    )


def whole_spec(shape):
    return pl.BlockSpec(shape, lambda i, *_: (0,) * len(shape))


def pack_first(sizes, roots, near, q, cour_all, diff_all):
    planes = q.shape[0] // C
    n = sizes["tile"]
    rows = 3 * planes + 8
    return pl.pallas_call(
        functools.partial(pack_kernel, sizes, planes),
        out_shape=jax.ShapeDtypeStruct((n, rows, C), jnp.float32),
        grid_spec=pltpu.PrefetchScalarGridSpec(
            num_scalar_prefetch=2,
            grid=(1,),
            in_specs=[
                whole_spec(q.shape),
                field_spec(0),
                field_spec(1),
                field_spec(0),
                field_spec(1),
            ],
            out_specs=whole_spec((n, rows, C)),
            scratch_shapes=[
                pltpu.VMEM((4, rows, C), jnp.float32),
                pltpu.VMEM((groups_of(planes) * C, C), jnp.float32),
            ],
        ),
        compiler_params=pltpu.CompilerParams(vmem_limit_bytes=VMEM_LIMIT),
        name="pack_first",
    )(roots, near, q, cour_all, cour_all, diff_all, diff_all)


def orientation(flipped):
    row = lax.broadcasted_iota(jnp.int32, (C, C), 0)
    col = lax.broadcasted_iota(jnp.int32, (C, C), 1)
    target = jnp.where(flipped == 1, C - 1 - row, row)
    return jnp.where(col == target, 1.0, 0.0).astype(jnp.float32)


def oriented(rows, turn):
    return jnp.dot(
        rows, turn, precision=lax.Precision.HIGHEST, preferred_element_type=jnp.float32
    )


def taps(c, k):
    s = jnp.abs(c)
    rest = 1.0 - s
    mid = c * rest * rest
    outer = -s * rest
    ahead = (3.0 - 2.0 * s) * s
    pos = jnp.maximum(c, 0.0)
    neg = jnp.minimum(c, 0.0)
    out_pos = pos * outer
    out_neg = neg * outer
    a = 7.0 / 12.0
    b = -1.0 / 12.0
    return [
        b * out_pos,
        b * mid + a * out_pos,
        a * (mid + out_pos) + b * out_neg + pos * ahead + k,
        a * (mid + out_neg) + b * out_pos + neg * ahead - k,
        b * mid + a * out_neg,
        b * out_neg,
    ]


def stencil(low, high):
    zero = [None]
    lo = low + zero
    hi = zero + high
    result = []
    for a, b in zip(lo, hi):
        result.append(-b if a is None else a if b is None else a - b)
    return result


def step_kernel(
    sizes, planes, k, last, roots, near, flips, q, cour, diff, got_faces, got, *rest
):
    if last:
        out, padded, turned, ghosts, coef, south, faces = rest
    else:
        out, slots, padded, turned, ghosts, coef, south, faces, strips = rest
    groups = groups_of(planes)

    @pl.loop(0, planes)
    def _(p):
        padded[pl.ds(pl.multiple_of(p * PAD + 8, 8), C), :] = q[
            pl.ds(pl.multiple_of(p * C, C), C), :
        ]

    for e in range(4):
        turn = orientation(flips[0, e])
        ghost = oriented(got[near[0, e]], turn)
        for d in range(3):
            part = ghost[d * planes : (d + 1) * planes]
            if e == 0:
                turned[pl.ds(2 - d, planes, stride=8), :] = part
            elif e == 1:
                turned[pl.ds(3 + d, planes, stride=8), :] = part
            elif e == 2:
                padded[pl.ds(7 - d, planes, stride=PAD), :] = part
            else:
                padded[pl.ds(C + 8 + d, planes, stride=PAD), :] = part
        if e in (1, 3):
            face = oriented(got_faces[near[0, e], pl.ds(3 * planes, 8), :], turn)
            if e == 1:
                faces[0:8, :] = face
            else:
                for t, field in enumerate((cour, diff)):
                    for lev in range(2):
                        j = (k * 2 + t) * 2 + lev
                        base = (t * 2 + lev) * (C + 8)
                        south[pl.ds(base, C), :] = field[0, 0, 1, lev]
                        south[pl.ds(base + C, 8), :] = jnp.broadcast_to(face[j : j + 1], (8, C))
    for g in range(groups):
        ghosts[pl.ds(g * C, C), :] = turned[pl.ds(g * C, C), :].T
    faces[...] = faces[...].T

    lane8 = lanes(8)

    @pl.loop(0, C // 8)
    def _(r):
        at = pl.multiple_of(r * 8, 8)
        east = faces[pl.ds(at, 8), :]
        for lev in range(2):
            low_x, high_x, low_y, high_y = [], [], [], []
            for t, field in enumerate((cour, diff)):
                j = (k * 2 + t) * 2 + lev
                west = field[0, 0, 0, lev, pl.ds(at, 8), :]
                low_x.append(west)
                high_x.append(
                    jnp.where(
                        lane8 == C - 1, pltpu.roll(east, C - 1 - j, 1), pltpu.roll(west, C - 1, 1)
                    )
                )
                base = (t * 2 + lev) * (C + 8)
                low_y.append(south[pl.ds(base + at, 8), :])
                high_y.append(south[pl.ds(base + at + 1, 8), :])
            along_x = stencil(taps(*low_x), taps(*high_x))
            along_y = stencil(taps(*low_y), taps(*high_y))
            centre = 1.0 + along_x[3] + along_y[3]
            every = [centre] + along_x[:3] + along_x[4:] + along_y[:3] + along_y[4:]
            for i, value in enumerate(every):
                coef[lev * 13 + i, pl.ds(at, 8), :] = value

    @pl.loop(0, C // 8)
    def _(r):
        at = pl.multiple_of(r * 8, 8)
        for lev in range(2):
            w = [coef[lev * 13 + i, pl.ds(at, 8), :] for i in range(13)]
            for s in range(planes // 2):
                p = 2 * s + lev
                base = p * PAD + 8 + at
                mid = padded[pl.ds(base, 8), :]
                edge = ghosts[pl.ds((p // 16) * C + at, 8), :]
                edge = pltpu.roll(edge, C - (8 * (p % 16) + 3), 1)
                total = w[0] * mid
                for i, d in enumerate((3, 2, 1)):
                    total += w[1 + i] * pltpu.roll(
                        jnp.where(lane8 >= C - d, edge, mid), d, 1
                    )
                    total += w[7 + i] * padded[pl.ds(base - d, 8), :]
                for i, d in enumerate((1, 2, 3)):
                    total += w[4 + i] * pltpu.roll(
                        jnp.where(lane8 < d, edge, mid), C - d, 1
                    )
                    total += w[10 + i] * padded[pl.ds(base + d, 8), :]
                out[pl.ds(p * C + at, 8), :] = total

    if not last:
        pack_strips(planes, out, strips, turned)
        fill_slots(sizes["tile"], near, strips, slots)


def advance(sizes, k, last, roots, near, flips, q, cour_all, diff_all, got_faces, got):
    planes = q.shape[0] // C
    n = sizes["tile"]
    rows = 3 * planes
    out_shape = [jax.ShapeDtypeStruct(q.shape, q.dtype)]
    out_specs = [whole_spec(q.shape)]
    groups = groups_of(planes)
    scratch = [
        pltpu.VMEM((planes * PAD, C), jnp.float32),
        pltpu.VMEM((groups * C, C), jnp.float32),
        pltpu.VMEM((groups * C, C), jnp.float32),
        pltpu.VMEM((26, C, C), jnp.float32),
        pltpu.VMEM((4 * (C + 8), C), jnp.float32),
        pltpu.VMEM((C, C), jnp.float32),
    ]
    if not last:
        out_shape.append(jax.ShapeDtypeStruct((n, rows, C), q.dtype))
        out_specs.append(whole_spec((n, rows, C)))
        scratch.append(pltpu.VMEM((4, rows, C), jnp.float32))
    return pl.pallas_call(
        functools.partial(step_kernel, sizes, planes, k, last),
        out_shape=out_shape,
        grid_spec=pltpu.PrefetchScalarGridSpec(
            num_scalar_prefetch=3,
            grid=(1,),
            in_specs=[
                whole_spec(q.shape),
                field_spec(k),
                field_spec(k),
                whole_spec(got_faces.shape),
                whole_spec(got.shape),
            ],
            out_specs=out_specs,
            scratch_shapes=scratch,
        ),
        compiler_params=pltpu.CompilerParams(vmem_limit_bytes=VMEM_LIMIT),
        name=f"advance_{k}",
    )(roots, near, flips, q, cour_all, diff_all, got_faces, got)


def body(sizes, tracers, courant, diffusivity, edge_blocks, edge_flips, roots):
    q = tracers.reshape(-1, C)
    cour_all, diff_all = spread_fields(sizes, courant, diffusivity)
    slots = pack_first(sizes, roots, edge_blocks, q, cour_all, diff_all)
    first = swap_slots(sizes, slots, 0)
    q, slots = advance(
        sizes, 0, False, roots, edge_blocks, edge_flips, q, cour_all, diff_all, first, first
    )
    second = swap_slots(sizes, slots, 1)
    (q,) = advance(
        sizes, 1, True, roots, edge_blocks, edge_flips, q, cour_all, diff_all, first, second
    )
    return q.reshape(tracers.shape)


def solution(mesh):
    placed = (
        P("spec", None, "tile", None),
        P("spec", None, None, None, "tile", None),
        P("spec", None, None, None, "tile", None),
        P("tile", None),
        P("tile", None),
        P(None, "tile"),
    )
    return jax.shard_map(
        functools.partial(body, dict(mesh.shape)),
        mesh=mesh,
        in_specs=placed,
        out_specs=P("spec", None, "tile", None),
        check_vma=False,
    )
```

```python
import functools
import math

import jax
import jax.numpy as jnp
from jax import lax
from jax.experimental import pallas as pl
from jax.experimental.pallas import tpu as pltpu
from jax.sharding import PartitionSpec as P

MESH = pl.DeviceIdType.MESH
C = 128
PAD = 144
VMEM_LIMIT = 56 * 1024 * 1024


def greet_all(sizes, axis):
    n = sizes[axis]
    me = lax.axis_index(axis)
    barrier = pltpu.get_barrier_semaphore()

    @pl.loop(1, n)
    def _(off):
        pl.semaphore_signal(
            barrier, inc=1, device_id={axis: lax.rem(me + off, n)}, device_id_type=MESH
        )

    pl.semaphore_wait(barrier, n - 1)


def spread_kernel(sizes, cour, diff, cour_all, diff_all, send_sem, recv_sem):
    n = sizes["spec"]
    me = lax.axis_index("spec")
    greet_all(sizes, "spec")

    def copies(off):
        peer = lax.rem(me + off, n)
        return [
            pltpu.make_async_remote_copy(
                src_ref=src.at[0],
                dst_ref=dst.at[me],
                send_sem=send_sem.at[which, off],
                recv_sem=recv_sem.at[which, off],
                device_id={"spec": peer},
                device_id_type=MESH,
            )
            for which, (src, dst) in enumerate([(cour, cour_all), (diff, diff_all)])
        ]

    @pl.loop(1, n)
    def _(off):
        for copy in copies(off):
            copy.start()

    @pl.loop(1, n)
    def _(off):
        for copy in copies(off):
            copy.wait()


def swap_kernel(sizes, slots, got, send_sem, recv_sem):
    n = sizes["tile"]
    me = lax.axis_index("tile")
    greet_all(sizes, "tile")

    def copy_to(off):
        peer = lax.rem(me + off, n)
        return pltpu.make_async_remote_copy(
            src_ref=slots.at[peer],
            dst_ref=got.at[me],
            send_sem=send_sem.at[off],
            recv_sem=recv_sem.at[off],
            device_id={"tile": peer},
            device_id_type=MESH,
        )

    @pl.loop(1, n)
    def _(off):
        copy_to(off).start()

    @pl.loop(1, n)
    def _(off):
        copy_to(off).wait()


def spread_fields(sizes, cour, diff):
    n = sizes["spec"]
    shape = jax.ShapeDtypeStruct((n,) + cour.shape[1:], cour.dtype)
    anywhere = pl.BlockSpec(memory_space=pl.ANY)
    return pl.pallas_call(
        functools.partial(spread_kernel, sizes),
        out_shape=(shape, shape),
        in_specs=[anywhere] * 2,
        out_specs=(anywhere, anywhere),
        scratch_shapes=[
            pltpu.SemaphoreType.DMA((2, n)),
            pltpu.SemaphoreType.DMA((2, n)),
        ],
        compiler_params=pltpu.CompilerParams(collective_id=0, has_side_effects=True),
        name="spread_fields",
    )(cour, diff)


def swap_slots(sizes, slots, which):
    n = sizes["tile"]
    anywhere = pl.BlockSpec(memory_space=pl.ANY)
    return pl.pallas_call(
        functools.partial(swap_kernel, sizes),
        out_shape=jax.ShapeDtypeStruct(slots.shape, slots.dtype),
        in_specs=[anywhere],
        out_specs=anywhere,
        scratch_shapes=[pltpu.SemaphoreType.DMA((n,)), pltpu.SemaphoreType.DMA((n,))],
        compiler_params=pltpu.CompilerParams(collective_id=1 + which, has_side_effects=True),
        name=f"swap_slots_{which}",
    )(slots)


def groups_of(planes):
    return -(-planes // 16)


def lanes(rows):
    return lax.broadcasted_iota(jnp.int32, (rows, C), 1)


def pack_strips(planes, q, strips, turned):
    lane_group = lanes(C) // 8
    for g in range(groups_of(planes)):
        packed = jnp.zeros((C, C), jnp.float32)
        for slot in range(min(16, planes - 16 * g)):
            plane = q[pl.ds((16 * g + slot) * C, C), :]
            packed = jnp.where(lane_group == slot, pltpu.roll(plane, 8 * slot + 3, 1), packed)
        turned[pl.ds(g * C, C), :] = packed.T
    for d in range(3):
        rows = pl.ds(d * planes, planes)
        strips[0, rows, :] = turned[pl.ds(3 + d, planes, stride=8), :]
        strips[1, rows, :] = turned[pl.ds(2 - d, planes, stride=8), :]
        strips[2, rows, :] = q[pl.ds(d, planes, stride=C), :]
        strips[3, rows, :] = q[pl.ds(C - 1 - d, planes, stride=C), :]


def fill_slots(n, near, strips, slots):
    @pl.loop(0, n)
    def _(dest):
        edge = jnp.int32(0)
        for e in range(1, 4):
            edge = jnp.where(near[0, e] == dest, e, edge)
        slots[dest] = strips[edge]


def pack_kernel(
    sizes, planes, roots, near, here, q, own_c, own_d, got_c0, got_c1, got_d0, got_d1,
    slots, fields, strips, turned
):
    pack_strips(planes, q, strips, turned)
    lane = lanes(C)
    faces = jnp.zeros((C, C), jnp.float32)
    for k, got in enumerate([(got_c0, got_d0), (got_c1, got_d1)]):
        mine = roots[k, 0] == here[0]
        for t, own in enumerate((own_c, own_d)):
            for lev in range(2):
                j = (k * 2 + t) * 2 + lev
                west = jnp.where(mine, own[0, k, 0, lev], got[t][0, 0, 0, lev])
                low = jnp.where(mine, own[0, k, 1, lev], got[t][0, 0, 1, lev])
                fields[k, t, 0, lev] = west
                fields[k, t, 1, lev] = low
                west = pltpu.roll(west, j, 1) if j else west
                faces = jnp.where(lane == j, west, faces)
                strips[2, pl.ds(3 * planes + j, 1), :] = low[0:1, :]
    strips[0, pl.ds(3 * planes, 8), :] = faces.T[0:8]
    strips[1, pl.ds(3 * planes, 8), :] = jnp.zeros((8, C), jnp.float32)
    strips[3, pl.ds(3 * planes, 8), :] = jnp.zeros((8, C), jnp.float32)
    fill_slots(sizes["tile"], near, strips, slots)


def field_spec(k):
    return pl.BlockSpec(
        (1, 1, 2, 2, C, C), lambda i, roots, *_: (roots[k, 0], k, 0, 0, 0, 0)
    )


def whole_spec(shape):
    return pl.BlockSpec(shape, lambda i, *_: (0,) * len(shape))


def pack_first(sizes, roots, near, q, cour, diff, cour_all, diff_all):
    planes = q.shape[0] // C
    n = sizes["tile"]
    rows = 3 * planes + 8
    return pl.pallas_call(
        functools.partial(pack_kernel, sizes, planes),
        out_shape=(
            jax.ShapeDtypeStruct((n, rows, C), jnp.float32),
            jax.ShapeDtypeStruct((2, 2, 2, 2, C, C), jnp.float32),
        ),
        grid_spec=pltpu.PrefetchScalarGridSpec(
            num_scalar_prefetch=3,
            grid=(1,),
            in_specs=[
                whole_spec(q.shape),
                whole_spec(cour.shape),
                whole_spec(diff.shape),
                field_spec(0),
                field_spec(1),
                field_spec(0),
                field_spec(1),
            ],
            out_specs=(whole_spec((n, rows, C)), whole_spec((2, 2, 2, 2, C, C))),
            scratch_shapes=[
                pltpu.VMEM((4, rows, C), jnp.float32),
                pltpu.VMEM((groups_of(planes) * C, C), jnp.float32),
            ],
        ),
        compiler_params=pltpu.CompilerParams(vmem_limit_bytes=VMEM_LIMIT),
        name="pack_first",
    )(
        roots,
        near,
        lax.axis_index("spec").reshape(1),
        q,
        cour,
        diff,
        cour_all,
        cour_all,
        diff_all,
        diff_all,
    )


def orientation(flipped):
    row = lax.broadcasted_iota(jnp.int32, (C, C), 0)
    col = lax.broadcasted_iota(jnp.int32, (C, C), 1)
    target = jnp.where(flipped == 1, C - 1 - row, row)
    return jnp.where(col == target, 1.0, 0.0).astype(jnp.float32)


def oriented(rows, turn):
    return jnp.dot(
        rows, turn, precision=lax.Precision.HIGHEST, preferred_element_type=jnp.float32
    )


def taps(c, k):
    s = jnp.abs(c)
    rest = 1.0 - s
    mid = c * rest * rest
    outer = -s * rest
    ahead = (3.0 - 2.0 * s) * s
    pos = jnp.maximum(c, 0.0)
    neg = jnp.minimum(c, 0.0)
    out_pos = pos * outer
    out_neg = neg * outer
    a = 7.0 / 12.0
    b = -1.0 / 12.0
    return [
        b * out_pos,
        b * mid + a * out_pos,
        a * (mid + out_pos) + b * out_neg + pos * ahead + k,
        a * (mid + out_neg) + b * out_pos + neg * ahead - k,
        b * mid + a * out_neg,
        b * out_neg,
    ]


def stencil(low, high):
    zero = [None]
    lo = low + zero
    hi = zero + high
    result = []
    for a, b in zip(lo, hi):
        result.append(-b if a is None else a if b is None else a - b)
    return result


def chunk_of(planes):
    return math.gcd(planes, 16)


SHIFTS = (-3, -2, -1, 1, 2, 3)


def shift_weights(weights):
    row = lax.broadcasted_iota(jnp.int32, (3 * C, C), 0)
    col = lax.broadcasted_iota(jnp.int32, (3 * C, C), 1)
    item = row & 7
    outside = jnp.where(item < 3, item - 3, C - 3 + item)
    outside = jnp.where((row < 2 * C + 16) & (item < 6), outside, -C)
    source = jnp.where(row < 2 * C, row & (C - 1), outside)
    for i, shift in enumerate(SHIFTS):
        weights[:, i * C : (i + 1) * C] = jnp.where(source == col + shift, 1.0, 0.0).astype(
            jnp.bfloat16
        )


def halves(x):
    big = x.astype(jnp.bfloat16)
    return big, (x - big.astype(jnp.float32)).astype(jnp.bfloat16)


def step_kernel(sizes, planes, k, last, near, flips, q, fields, got_faces, got, *rest):
    if last:
        out, padded, turned, coef, south, faces, split, weights, moved = rest
    else:
        out, slots, padded, turned, coef, south, faces, split, weights, moved, strips = rest
    groups = groups_of(planes)
    chunk = chunk_of(planes)
    shift_weights(weights)

    @pl.loop(0, planes)
    def _(p):
        at = pl.multiple_of(p * C, C)
        plane = q[pl.ds(at, C), :]
        padded[pl.ds(pl.multiple_of(p * PAD + 8, 8), C), :] = plane
        big, small = halves(plane)
        split[pl.ds(at, C), 0:C] = big
        split[pl.ds(at, C), C : 2 * C] = small

    turned[...] = jnp.zeros_like(turned)
    for e in range(4):
        turn = orientation(flips[0, e])
        ghost = oriented(got[near[0, e]], turn)
        for d in range(3):
            part = ghost[d * planes : (d + 1) * planes]
            if e == 0:
                turned[pl.ds(2 - d, planes, stride=8), :] = part
            elif e == 1:
                turned[pl.ds(3 + d, planes, stride=8), :] = part
            elif e == 2:
                padded[pl.ds(7 - d, planes, stride=PAD), :] = part
            else:
                padded[pl.ds(C + 8 + d, planes, stride=PAD), :] = part
        if e in (1, 3):
            face = oriented(got_faces[near[0, e], pl.ds(3 * planes, 8), :], turn)
            if e == 1:
                faces[...] = jnp.zeros_like(faces)
                faces[0:8, :] = face
            else:
                for t in range(2):
                    for lev in range(2):
                        j = (k * 2 + t) * 2 + lev
                        base = (t * 2 + lev) * (C + 8)
                        south[pl.ds(base, C), :] = fields[0, t, 1, lev]
                        south[pl.ds(base + C, 8), :] = jnp.broadcast_to(face[j : j + 1], (8, C))
    faces[...] = faces[...].T

    row = lax.broadcasted_iota(jnp.int32, (2 * C, C), 0)
    col = lax.broadcasted_iota(jnp.int32, (2 * C, C), 1)
    source = (row & 7) + 8 * (row // C)
    ghosts = [
        jnp.concatenate(halves(turned[pl.ds(g * C, C), :].T), axis=1) for g in range(groups)
    ]
    for slot in range(min(16, planes)):
        place = jnp.where((((row & (C - 1)) >> 3) == slot) & (source == col), 1.0, 0.0)
        place = place.astype(jnp.bfloat16)
        for g in range(groups):
            p = 16 * g + slot
            if p < planes:
                split[pl.ds(p * C, C), 2 * C : 3 * C] = jnp.dot(
                    ghosts[g], place, preferred_element_type=jnp.float32
                ).astype(jnp.bfloat16)

    lane8 = lanes(8)

    @pl.loop(0, C // 8)
    def _(r):
        at = pl.multiple_of(r * 8, 8)
        east = faces[pl.ds(at, 8), :]
        for lev in range(2):
            low_x, high_x, low_y, high_y = [], [], [], []
            for t in range(2):
                j = (k * 2 + t) * 2 + lev
                west = fields[0, t, 0, lev, pl.ds(at, 8), :]
                low_x.append(west)
                high_x.append(
                    jnp.where(
                        lane8 == C - 1, pltpu.roll(east, C - 1 - j, 1), pltpu.roll(west, C - 1, 1)
                    )
                )
                base = (t * 2 + lev) * (C + 8)
                low_y.append(south[pl.ds(base + at, 8), :])
                high_y.append(south[pl.ds(base + at + 1, 8), :])
            along_x = stencil(taps(*low_x), taps(*high_x))
            along_y = stencil(taps(*low_y), taps(*high_y))
            centre = 1.0 + along_x[3] + along_y[3]
            every = [centre] + along_x[:3] + along_x[4:] + along_y[:3] + along_y[4:]
            for i, value in enumerate(every):
                coef[lev * 13 + i, pl.ds(at, 8), :] = value

    @pl.loop(0, planes // chunk)
    def _(part):
        rows = min(4, chunk) * C

        @pl.loop(0, chunk * C // rows)
        def _(b):
            at = pl.multiple_of(part * (chunk * C) + b * rows, C)
            moved[pl.ds(pl.multiple_of(b * rows, C), rows), :] = jnp.dot(
                split[pl.ds(at, rows), :], weights[...], preferred_element_type=jnp.float32
            )

        @pl.loop(0, C // 8)
        def _(r):
            at = pl.multiple_of(r * 8, 8)
            for lev in range(2):
                w = [coef[lev * 13 + i, pl.ds(at, 8), :] for i in range(13)]
                for s in range(chunk // 2):
                    p = 2 * s + lev
                    base = (part * chunk + p) * PAD + 8 + at
                    here = pl.ds(pl.multiple_of(p * C + at, 8), 8)
                    total = w[0] * padded[pl.ds(base, 8), :]
                    for i, d in enumerate(SHIFTS):
                        total += w[1 + i] * moved[here, i * C : (i + 1) * C]
                        total += w[7 + i] * padded[pl.ds(base + d, 8), :]
                    to = pl.multiple_of((part * chunk + p) * C + at, 8)
                    out[pl.ds(to, 8), :] = total

    if not last:
        pack_strips(planes, out, strips, turned)
        fill_slots(sizes["tile"], near, strips, slots)


def advance(sizes, k, last, near, flips, q, fields, got_faces, got):
    planes = q.shape[0] // C
    n = sizes["tile"]
    rows = 3 * planes
    out_shape = [jax.ShapeDtypeStruct(q.shape, q.dtype)]
    out_specs = [whole_spec(q.shape)]
    groups = groups_of(planes)
    scratch = [
        pltpu.VMEM((planes * PAD, C), jnp.float32),
        pltpu.VMEM((groups * C, C), jnp.float32),
        pltpu.VMEM((26, C, C), jnp.float32),
        pltpu.VMEM((4 * (C + 8), C), jnp.float32),
        pltpu.VMEM((C, C), jnp.float32),
        pltpu.VMEM((planes * C, 3 * C), jnp.bfloat16),
        pltpu.VMEM((3 * C, 6 * C), jnp.bfloat16),
        pltpu.VMEM((chunk_of(planes) * C, 6 * C), jnp.float32),
    ]
    if not last:
        out_shape.append(jax.ShapeDtypeStruct((n, rows, C), q.dtype))
        out_specs.append(whole_spec((n, rows, C)))
        scratch.append(pltpu.VMEM((4, rows, C), jnp.float32))
    return pl.pallas_call(
        functools.partial(step_kernel, sizes, planes, k, last),
        out_shape=out_shape,
        grid_spec=pltpu.PrefetchScalarGridSpec(
            num_scalar_prefetch=2,
            grid=(1,),
            in_specs=[
                whole_spec(q.shape),
                pl.BlockSpec((1, 2, 2, 2, C, C), lambda i, *_: (k, 0, 0, 0, 0, 0)),
                whole_spec(got_faces.shape),
                whole_spec(got.shape),
            ],
            out_specs=out_specs,
            scratch_shapes=scratch,
        ),
        compiler_params=pltpu.CompilerParams(vmem_limit_bytes=VMEM_LIMIT),
        name=f"advance_{k}",
    )(near, flips, q, fields, got_faces, got)


def body(sizes, tracers, courant, diffusivity, edge_blocks, edge_flips, roots):
    q = tracers.reshape(-1, C)
    cour_all, diff_all = spread_fields(sizes, courant, diffusivity)
    slots, fields = pack_first(
        sizes, roots, edge_blocks, q, courant, diffusivity, cour_all, diff_all
    )
    first = swap_slots(sizes, slots, 0)
    q, slots = advance(sizes, 0, False, edge_blocks, edge_flips, q, fields, first, first)
    second = swap_slots(sizes, slots, 1)
    (q,) = advance(sizes, 1, True, edge_blocks, edge_flips, q, fields, first, second)
    return q.reshape(tracers.shape)


def solution(mesh):
    placed = (
        P("spec", None, "tile", None),
        P("spec", None, None, None, "tile", None),
        P("spec", None, None, None, "tile", None),
        P("tile", None),
        P("tile", None),
        P(None, "tile"),
    )
    return jax.shard_map(
        functools.partial(body, dict(mesh.shape)),
        mesh=mesh,
        in_specs=placed,
        out_specs=P("spec", None, "tile", None),
        check_vma=False,
    )
```

```python
import functools
import math

import jax
import jax.numpy as jnp
from jax import lax
from jax.experimental import pallas as pl
from jax.experimental.pallas import tpu as pltpu
from jax.sharding import PartitionSpec as P

MESH = pl.DeviceIdType.MESH
C = 128
PAD = 144
VMEM_LIMIT = 56 * 1024 * 1024


def greet_all(sizes, axis):
    n = sizes[axis]
    me = lax.axis_index(axis)
    barrier = pltpu.get_barrier_semaphore()

    @pl.loop(1, n)
    def _(off):
        pl.semaphore_signal(
            barrier, inc=1, device_id={axis: lax.rem(me + off, n)}, device_id_type=MESH
        )

    pl.semaphore_wait(barrier, n - 1)


def spread_kernel(sizes, cour, diff, cour_all, diff_all, send_sem, recv_sem):
    n = sizes["spec"]
    me = lax.axis_index("spec")
    greet_all(sizes, "spec")

    def copies(off):
        peer = lax.rem(me + off, n)
        return [
            pltpu.make_async_remote_copy(
                src_ref=src.at[0],
                dst_ref=dst.at[me],
                send_sem=send_sem.at[which, off],
                recv_sem=recv_sem.at[which, off],
                device_id={"spec": peer},
                device_id_type=MESH,
            )
            for which, (src, dst) in enumerate([(cour, cour_all), (diff, diff_all)])
        ]

    @pl.loop(1, n)
    def _(off):
        for copy in copies(off):
            copy.start()

    @pl.loop(1, n)
    def _(off):
        for copy in copies(off):
            copy.wait()


def swap_kernel(
    sizes, slots, strips, got, theirs, relay, far_sem, send_sem, recv_sem, send_on, recv_on, own_sem
):
    n = sizes["tile"]
    half = n // 2
    rows = slots.shape[1]
    me = lax.axis_index("tile")
    place = lax.rem(me, half)
    base = me - place
    far = lax.rem(me + half, n)
    barrier = pltpu.get_barrier_semaphore()
    pl.semaphore_signal(barrier, inc=1, device_id={"tile": far}, device_id_type=MESH)

    @pl.loop(1, half)
    def _(off):
        pl.semaphore_signal(
            barrier,
            inc=1,
            device_id={"tile": base + lax.rem(place + off, half)},
            device_id_type=MESH,
        )

    pl.semaphore_wait(barrier, half)

    across = pltpu.make_async_remote_copy(
        src_ref=strips,
        dst_ref=theirs,
        send_sem=far_sem.at[0],
        recv_sem=far_sem.at[1],
        device_id={"tile": far},
        device_id_type=MESH,
    )

    def direct(off):
        to = lax.rem(place + off, half)
        return pltpu.make_async_remote_copy(
            src_ref=slots.at[to],
            dst_ref=got.at[me],
            send_sem=send_sem.at[off],
            recv_sem=recv_sem.at[off],
            device_id={"tile": base + to},
            device_id_type=MESH,
        )

    def onward(off):
        to = lax.rem(place + off, half)
        return pltpu.make_async_remote_copy(
            src_ref=relay.at[to],
            dst_ref=got.at[far],
            send_sem=send_on.at[off],
            recv_sem=recv_on.at[off],
            device_id={"tile": base + to},
            device_id_type=MESH,
        )

    def choose(to):
        wanted = (base + to).astype(jnp.float32)
        masks = [theirs[e, pl.ds(rows, 8), :] == wanted for e in range(1, 4)]

        @pl.loop(0, rows // 8)
        def _(r):
            at = pl.ds(pl.multiple_of(r * 8, 8), 8)
            value = theirs[0, at, :]
            for e, mask in enumerate(masks):
                value = jnp.where(mask, theirs[e + 1, at, :], value)
            relay[to, at, :] = value

    across.start()

    @pl.loop(1, half)
    def _(off):
        direct(off).start()

    across.wait_recv()

    @pl.loop(1, half)
    def _(off):
        choose(lax.rem(place + off, half))
        onward(off).start()

    choose(place)
    own = pltpu.make_async_copy(relay.at[place], got.at[far], own_sem)
    own.start()
    across.wait_send()

    @pl.loop(1, half)
    def _(off):
        direct(off).wait()
        onward(off).wait()

    own.wait()


def spread_fields(sizes, cour, diff):
    n = sizes["spec"]
    shape = jax.ShapeDtypeStruct((n,) + cour.shape[1:], cour.dtype)
    anywhere = pl.BlockSpec(memory_space=pl.ANY)
    return pl.pallas_call(
        functools.partial(spread_kernel, sizes),
        out_shape=(shape, shape),
        in_specs=[anywhere] * 2,
        out_specs=(anywhere, anywhere),
        scratch_shapes=[
            pltpu.SemaphoreType.DMA((2, n)),
            pltpu.SemaphoreType.DMA((2, n)),
        ],
        compiler_params=pltpu.CompilerParams(collective_id=0, has_side_effects=True),
        name="spread_fields",
    )(cour, diff)


def swap_slots(sizes, slots, strips, which):
    n = sizes["tile"]
    half, rows = slots.shape[0], slots.shape[1]
    anywhere = pl.BlockSpec(memory_space=pl.ANY)
    return pl.pallas_call(
        functools.partial(swap_kernel, sizes),
        out_shape=jax.ShapeDtypeStruct((n, rows, C), slots.dtype),
        in_specs=[anywhere, anywhere],
        out_specs=anywhere,
        scratch_shapes=[
            pltpu.VMEM(strips.shape, jnp.float32),
            pltpu.VMEM(slots.shape, jnp.float32),
            pltpu.SemaphoreType.DMA((2,)),
            pltpu.SemaphoreType.DMA((half,)),
            pltpu.SemaphoreType.DMA((half,)),
            pltpu.SemaphoreType.DMA((half,)),
            pltpu.SemaphoreType.DMA((half,)),
            pltpu.SemaphoreType.DMA,
        ],
        compiler_params=pltpu.CompilerParams(collective_id=1 + which, has_side_effects=True),
        name=f"swap_slots_{which}",
    )(slots, strips)


def rows_of(planes, faces):
    return -(-(3 * planes + faces) // 8) * 8


def groups_of(planes):
    return -(-planes // 16)


def lanes(rows):
    return lax.broadcasted_iota(jnp.int32, (rows, C), 1)


def pack_strips(planes, q, strips, turned):
    lane_group = lanes(C) // 8
    for g in range(groups_of(planes)):
        packed = jnp.zeros((C, C), jnp.float32)
        for slot in range(min(16, planes - 16 * g)):
            plane = q[pl.ds((16 * g + slot) * C, C), :]
            packed = jnp.where(lane_group == slot, pltpu.roll(plane, 8 * slot + 3, 1), packed)
        turned[pl.ds(g * C, C), :] = packed.T
    for d in range(3):
        rows = pl.ds(d * planes, planes)
        strips[0, rows, :] = turned[pl.ds(3 + d, planes, stride=8), :]
        strips[1, rows, :] = turned[pl.ds(2 - d, planes, stride=8), :]
        strips[2, rows, :] = q[pl.ds(d, planes, stride=C), :]
        strips[3, rows, :] = q[pl.ds(C - 1 - d, planes, stride=C), :]


def fill_slots(near, here, strips, slots):
    rows = slots.shape[1]
    for e in range(4):
        owner = near[0, e].astype(jnp.float32)
        strips[e, pl.ds(rows, 8), :] = jnp.full((8, C), owner, jnp.float32)

    @pl.loop(0, slots.shape[0])
    def _(i):
        dest = here[1] + i
        edge = jnp.int32(0)
        for e in range(1, 4):
            edge = jnp.where(near[0, e] == dest, e, edge)
        slots[i] = strips[edge, pl.ds(0, rows), :]


def pack_kernel(
    sizes, planes, roots, near, here, q, own_c, own_d, got_c0, got_c1, got_d0, got_d1,
    slots, strips, fields, turned
):
    pack_strips(planes, q, strips, turned)
    lane = lanes(C)
    faces = jnp.zeros((C, C), jnp.float32)
    for k, got in enumerate([(got_c0, got_d0), (got_c1, got_d1)]):
        mine = roots[k, 0] == here[0]
        for t, own in enumerate((own_c, own_d)):
            for lev in range(2):
                j = (k * 2 + t) * 2 + lev
                west = jnp.where(mine, own[0, k, 0, lev], got[t][0, 0, 0, lev])
                low = jnp.where(mine, own[0, k, 1, lev], got[t][0, 0, 1, lev])
                fields[k, t, 0, lev] = west
                fields[k, t, 1, lev] = low
                west = pltpu.roll(west, j, 1) if j else west
                faces = jnp.where(lane == j, west, faces)
                strips[2, pl.ds(3 * planes + j, 1), :] = low[0:1, :]
    strips[0, pl.ds(3 * planes, 8), :] = faces.T[0:8]
    strips[1, pl.ds(3 * planes, 8), :] = jnp.zeros((8, C), jnp.float32)
    strips[3, pl.ds(3 * planes, 8), :] = jnp.zeros((8, C), jnp.float32)
    fill_slots(near, here, strips, slots)


def field_spec(k):
    return pl.BlockSpec(
        (1, 1, 2, 2, C, C), lambda i, roots, *_: (roots[k, 0], k, 0, 0, 0, 0)
    )


def whole_spec(shape):
    return pl.BlockSpec(shape, lambda i, *_: (0,) * len(shape))


def pack_first(sizes, roots, near, here, q, cour, diff, cour_all, diff_all):
    planes = q.shape[0] // C
    half = sizes["tile"] // 2
    rows = rows_of(planes, 8)
    return pl.pallas_call(
        functools.partial(pack_kernel, sizes, planes),
        out_shape=(
            jax.ShapeDtypeStruct((half, rows, C), jnp.float32),
            jax.ShapeDtypeStruct((4, rows + 8, C), jnp.float32),
            jax.ShapeDtypeStruct((2, 2, 2, 2, C, C), jnp.float32),
        ),
        grid_spec=pltpu.PrefetchScalarGridSpec(
            num_scalar_prefetch=3,
            grid=(1,),
            in_specs=[
                whole_spec(q.shape),
                whole_spec(cour.shape),
                whole_spec(diff.shape),
                field_spec(0),
                field_spec(1),
                field_spec(0),
                field_spec(1),
            ],
            out_specs=(
                whole_spec((half, rows, C)),
                whole_spec((4, rows + 8, C)),
                whole_spec((2, 2, 2, 2, C, C)),
            ),
            scratch_shapes=[
                pltpu.VMEM((groups_of(planes) * C, C), jnp.float32),
            ],
        ),
        compiler_params=pltpu.CompilerParams(vmem_limit_bytes=VMEM_LIMIT),
        name="pack_first",
    )(
        roots,
        near,
        here,
        q,
        cour,
        diff,
        cour_all,
        cour_all,
        diff_all,
        diff_all,
    )


def orientation(flipped):
    row = lax.broadcasted_iota(jnp.int32, (C, C), 0)
    col = lax.broadcasted_iota(jnp.int32, (C, C), 1)
    target = jnp.where(flipped == 1, C - 1 - row, row)
    return jnp.where(col == target, 1.0, 0.0).astype(jnp.float32)


def oriented(rows, turn):
    return jnp.dot(
        rows, turn, precision=lax.Precision.HIGHEST, preferred_element_type=jnp.float32
    )


def taps(c, k):
    s = jnp.abs(c)
    rest = 1.0 - s
    mid = c * rest * rest
    outer = -s * rest
    ahead = (3.0 - 2.0 * s) * s
    pos = jnp.maximum(c, 0.0)
    neg = jnp.minimum(c, 0.0)
    out_pos = pos * outer
    out_neg = neg * outer
    a = 7.0 / 12.0
    b = -1.0 / 12.0
    return [
        b * out_pos,
        b * mid + a * out_pos,
        a * (mid + out_pos) + b * out_neg + pos * ahead + k,
        a * (mid + out_neg) + b * out_pos + neg * ahead - k,
        b * mid + a * out_neg,
        b * out_neg,
    ]


def stencil(low, high):
    zero = [None]
    lo = low + zero
    hi = zero + high
    result = []
    for a, b in zip(lo, hi):
        result.append(-b if a is None else a if b is None else a - b)
    return result


def chunk_of(planes):
    return math.gcd(planes, 16)


SHIFTS = (-3, -2, -1, 1, 2, 3)


def shift_weights(weights):
    row = lax.broadcasted_iota(jnp.int32, (3 * C, C), 0)
    col = lax.broadcasted_iota(jnp.int32, (3 * C, C), 1)
    item = row & 7
    outside = jnp.where(item < 3, item - 3, C - 3 + item)
    outside = jnp.where((row < 2 * C + 16) & (item < 6), outside, -C)
    source = jnp.where(row < 2 * C, row & (C - 1), outside)
    for i, shift in enumerate(SHIFTS):
        weights[:, i * C : (i + 1) * C] = jnp.where(source == col + shift, 1.0, 0.0).astype(
            jnp.bfloat16
        )


def halves(x):
    big = x.astype(jnp.bfloat16)
    return big, (x - big.astype(jnp.float32)).astype(jnp.bfloat16)


def step_kernel(sizes, planes, k, last, near, flips, here, q, fields, got_faces, got, *rest):
    if last:
        out, padded, turned, coef, south, faces, split, weights, moved = rest
    else:
        out, slots, strips, padded, turned, coef, south, faces, split, weights, moved = rest
    groups = groups_of(planes)
    chunk = chunk_of(planes)
    shift_weights(weights)

    @pl.loop(0, planes)
    def _(p):
        at = pl.multiple_of(p * C, C)
        plane = q[pl.ds(at, C), :]
        padded[pl.ds(pl.multiple_of(p * PAD + 8, 8), C), :] = plane
        big, small = halves(plane)
        split[pl.ds(at, C), 0:C] = big
        split[pl.ds(at, C), C : 2 * C] = small

    turned[...] = jnp.zeros_like(turned)
    for e in range(4):
        turn = orientation(flips[0, e])
        ghost = oriented(got[near[0, e]], turn)
        for d in range(3):
            part = ghost[d * planes : (d + 1) * planes]
            if e == 0:
                turned[pl.ds(2 - d, planes, stride=8), :] = part
            elif e == 1:
                turned[pl.ds(3 + d, planes, stride=8), :] = part
            elif e == 2:
                padded[pl.ds(7 - d, planes, stride=PAD), :] = part
            else:
                padded[pl.ds(C + 8 + d, planes, stride=PAD), :] = part
        if e in (1, 3):
            face = oriented(got_faces[near[0, e], pl.ds(3 * planes, 8), :], turn)
            if e == 1:
                faces[...] = jnp.zeros_like(faces)
                faces[0:8, :] = face
            else:
                for t in range(2):
                    for lev in range(2):
                        j = (k * 2 + t) * 2 + lev
                        base = (t * 2 + lev) * (C + 8)
                        south[pl.ds(base, C), :] = fields[0, t, 1, lev]
                        south[pl.ds(base + C, 8), :] = jnp.broadcast_to(face[j : j + 1], (8, C))
    faces[...] = faces[...].T

    row = lax.broadcasted_iota(jnp.int32, (2 * C, C), 0)
    col = lax.broadcasted_iota(jnp.int32, (2 * C, C), 1)
    source = (row & 7) + 8 * (row // C)
    ghosts = [
        jnp.concatenate(halves(turned[pl.ds(g * C, C), :].T), axis=1) for g in range(groups)
    ]
    for slot in range(min(16, planes)):
        place = jnp.where((((row & (C - 1)) >> 3) == slot) & (source == col), 1.0, 0.0)
        place = place.astype(jnp.bfloat16)
        for g in range(groups):
            p = 16 * g + slot
            if p < planes:
                split[pl.ds(p * C, C), 2 * C : 3 * C] = jnp.dot(
                    ghosts[g], place, preferred_element_type=jnp.float32
                ).astype(jnp.bfloat16)

    lane8 = lanes(8)

    @pl.loop(0, C // 8)
    def _(r):
        at = pl.multiple_of(r * 8, 8)
        east = faces[pl.ds(at, 8), :]
        for lev in range(2):
            low_x, high_x, low_y, high_y = [], [], [], []
            for t in range(2):
                j = (k * 2 + t) * 2 + lev
                west = fields[0, t, 0, lev, pl.ds(at, 8), :]
                low_x.append(west)
                high_x.append(
                    jnp.where(
                        lane8 == C - 1, pltpu.roll(east, C - 1 - j, 1), pltpu.roll(west, C - 1, 1)
                    )
                )
                base = (t * 2 + lev) * (C + 8)
                low_y.append(south[pl.ds(base + at, 8), :])
                high_y.append(south[pl.ds(base + at + 1, 8), :])
            along_x = stencil(taps(*low_x), taps(*high_x))
            along_y = stencil(taps(*low_y), taps(*high_y))
            centre = 1.0 + along_x[3] + along_y[3]
            every = [centre] + along_x[:3] + along_x[4:] + along_y[:3] + along_y[4:]
            for i, value in enumerate(every):
                coef[lev * 13 + i, pl.ds(at, 8), :] = value

    @pl.loop(0, planes // chunk)
    def _(part):
        rows = min(4, chunk) * C

        @pl.loop(0, chunk * C // rows)
        def _(b):
            at = pl.multiple_of(part * (chunk * C) + b * rows, C)
            moved[pl.ds(pl.multiple_of(b * rows, C), rows), :] = jnp.dot(
                split[pl.ds(at, rows), :], weights[...], preferred_element_type=jnp.float32
            )

        @pl.loop(0, C // 8)
        def _(r):
            at = pl.multiple_of(r * 8, 8)
            for lev in range(2):
                w = [coef[lev * 13 + i, pl.ds(at, 8), :] for i in range(13)]
                for s in range(chunk // 2):
                    p = 2 * s + lev
                    base = (part * chunk + p) * PAD + 8 + at
                    here = pl.ds(pl.multiple_of(p * C + at, 8), 8)
                    total = w[0] * padded[pl.ds(base, 8), :]
                    for i, d in enumerate(SHIFTS):
                        total += w[1 + i] * moved[here, i * C : (i + 1) * C]
                        total += w[7 + i] * padded[pl.ds(base + d, 8), :]
                    to = pl.multiple_of((part * chunk + p) * C + at, 8)
                    out[pl.ds(to, 8), :] = total

    if not last:
        pack_strips(planes, out, strips, turned)
        fill_slots(near, here, strips, slots)


def advance(sizes, k, last, near, flips, here, q, fields, got_faces, got):
    planes = q.shape[0] // C
    half = sizes["tile"] // 2
    rows = rows_of(planes, 0)
    out_shape = [jax.ShapeDtypeStruct(q.shape, q.dtype)]
    out_specs = [whole_spec(q.shape)]
    groups = groups_of(planes)
    scratch = [
        pltpu.VMEM((planes * PAD, C), jnp.float32),
        pltpu.VMEM((groups * C, C), jnp.float32),
        pltpu.VMEM((26, C, C), jnp.float32),
        pltpu.VMEM((4 * (C + 8), C), jnp.float32),
        pltpu.VMEM((C, C), jnp.float32),
        pltpu.VMEM((planes * C, 3 * C), jnp.bfloat16),
        pltpu.VMEM((3 * C, 6 * C), jnp.bfloat16),
        pltpu.VMEM((chunk_of(planes) * C, 6 * C), jnp.float32),
    ]
    if not last:
        for shape in ((half, rows, C), (4, rows + 8, C)):
            out_shape.append(jax.ShapeDtypeStruct(shape, q.dtype))
            out_specs.append(whole_spec(shape))
    return pl.pallas_call(
        functools.partial(step_kernel, sizes, planes, k, last),
        out_shape=out_shape,
        grid_spec=pltpu.PrefetchScalarGridSpec(
            num_scalar_prefetch=3,
            grid=(1,),
            in_specs=[
                whole_spec(q.shape),
                pl.BlockSpec((1, 2, 2, 2, C, C), lambda i, *_: (k, 0, 0, 0, 0, 0)),
                whole_spec(got_faces.shape),
                whole_spec(got.shape),
            ],
            out_specs=out_specs,
            scratch_shapes=scratch,
        ),
        compiler_params=pltpu.CompilerParams(vmem_limit_bytes=VMEM_LIMIT),
        name=f"advance_{k}",
    )(near, flips, here, q, fields, got_faces, got)


def body(sizes, tracers, courant, diffusivity, edge_blocks, edge_flips, roots):
    q = tracers.reshape(-1, C)
    cour_all, diff_all = spread_fields(sizes, courant, diffusivity)
    half = sizes["tile"] // 2
    here = jnp.stack([lax.axis_index("spec"), lax.axis_index("tile") // half * half])
    slots, strips, fields = pack_first(
        sizes, roots, edge_blocks, here, q, courant, diffusivity, cour_all, diff_all
    )
    first = swap_slots(sizes, slots, strips, 0)
    block = (edge_blocks, edge_flips, here)
    q, slots, strips = advance(sizes, 0, False, *block, q, fields, first, first)
    second = swap_slots(sizes, slots, strips, 1)
    (q,) = advance(sizes, 1, True, *block, q, fields, first, second)
    return q.reshape(tracers.shape)


def solution(mesh):
    placed = (
        P("spec", None, "tile", None),
        P("spec", None, None, None, "tile", None),
        P("spec", None, None, None, "tile", None),
        P("tile", None),
        P("tile", None),
        P(None, "tile"),
    )
    return jax.shard_map(
        functools.partial(body, dict(mesh.shape)),
        mesh=mesh,
        in_specs=placed,
        out_specs=P("spec", None, "tile", None),
        check_vma=False,
    )
```

```python
import functools
import math

import jax
import jax.numpy as jnp
from jax import lax
from jax.experimental import pallas as pl
from jax.experimental.pallas import tpu as pltpu
from jax.sharding import PartitionSpec as P

MESH = pl.DeviceIdType.MESH
C = 128
PAD = 144
VMEM_LIMIT = 56 * 1024 * 1024


def greet_all(sizes, axis):
    n = sizes[axis]
    me = lax.axis_index(axis)
    barrier = pltpu.get_barrier_semaphore()

    @pl.loop(1, n)
    def _(off):
        pl.semaphore_signal(
            barrier, inc=1, device_id={axis: lax.rem(me + off, n)}, device_id_type=MESH
        )

    pl.semaphore_wait(barrier, n - 1)


def spread_kernel(sizes, cour, diff, cour_all, diff_all, send_sem, recv_sem):
    n = sizes["spec"]
    me = lax.axis_index("spec")
    greet_all(sizes, "spec")

    def copies(off):
        peer = lax.rem(me + off, n)
        return [
            pltpu.make_async_remote_copy(
                src_ref=src.at[0],
                dst_ref=dst.at[me],
                send_sem=send_sem.at[which, off],
                recv_sem=recv_sem.at[which, off],
                device_id={"spec": peer},
                device_id_type=MESH,
            )
            for which, (src, dst) in enumerate([(cour, cour_all), (diff, diff_all)])
        ]

    @pl.loop(1, n)
    def _(off):
        for copy in copies(off):
            copy.start()

    @pl.loop(1, n)
    def _(off):
        for copy in copies(off):
            copy.wait()


def swap_kernel(
    sizes, slots, strips, got, theirs, relay, far_sem, send_sem, recv_sem, send_on, recv_on, own_sem
):
    n = sizes["tile"]
    half = n // 2
    rows = slots.shape[1]
    me = lax.axis_index("tile")
    place = lax.rem(me, half)
    base = me - place
    far = lax.rem(me + half, n)
    barrier = pltpu.get_barrier_semaphore()
    pl.semaphore_signal(barrier, inc=1, device_id={"tile": far}, device_id_type=MESH)

    @pl.loop(1, half)
    def _(off):
        pl.semaphore_signal(
            barrier,
            inc=1,
            device_id={"tile": base + lax.rem(place + off, half)},
            device_id_type=MESH,
        )

    pl.semaphore_wait(barrier, half)

    cut = rows // 16 * 8
    pieces = ((cut, rows - cut, 8), (0, cut, 0))

    def across(piece):
        first, count, extra = pieces[piece]
        part = pl.ds(first, count + extra)
        return pltpu.make_async_remote_copy(
            src_ref=strips.at[:, part, :],
            dst_ref=theirs.at[:, part, :],
            send_sem=far_sem.at[0, piece],
            recv_sem=far_sem.at[1, piece],
            device_id={"tile": far},
            device_id_type=MESH,
        )

    def direct(off):
        to = lax.rem(place + off, half)
        return pltpu.make_async_remote_copy(
            src_ref=slots.at[to],
            dst_ref=got.at[me],
            send_sem=send_sem.at[off],
            recv_sem=recv_sem.at[off],
            device_id={"tile": base + to},
            device_id_type=MESH,
        )

    def onward(piece, off):
        to = lax.rem(place + off, half)
        part = pl.ds(*pieces[piece][:2])
        return pltpu.make_async_remote_copy(
            src_ref=relay.at[to, part, :],
            dst_ref=got.at[far, part, :],
            send_sem=send_on.at[piece, off],
            recv_sem=recv_on.at[piece, off],
            device_id={"tile": base + to},
            device_id_type=MESH,
        )

    def choose(piece, to):
        first, count, _ = pieces[piece]
        wanted = (base + to).astype(jnp.float32)
        masks = [theirs[e, pl.ds(rows, 8), :] == wanted for e in range(1, 4)]

        @pl.loop(0, count // 8)
        def _(r):
            at = pl.ds(pl.multiple_of(first + r * 8, 8), 8)
            value = theirs[0, at, :]
            for e, mask in enumerate(masks):
                value = jnp.where(mask, theirs[e + 1, at, :], value)
            relay[to, at, :] = value

    for piece in range(2):
        across(piece).start()

    @pl.loop(1, half)
    def _(off):
        direct(off).start()

    for piece in range(2):
        across(piece).wait_recv()

        @pl.loop(1, half)
        def _(off):
            choose(piece, lax.rem(place + off, half))
            onward(piece, off).start()

    for piece in range(2):
        choose(piece, place)
    own = pltpu.make_async_copy(relay.at[place], got.at[far], own_sem)
    own.start()

    for piece in range(2):
        across(piece).wait_send()

    @pl.loop(1, half)
    def _(off):
        direct(off).wait()
        for piece in range(2):
            onward(piece, off).wait()

    own.wait()


def spread_fields(sizes, cour, diff):
    n = sizes["spec"]
    shape = jax.ShapeDtypeStruct((n,) + cour.shape[1:], cour.dtype)
    anywhere = pl.BlockSpec(memory_space=pl.ANY)
    return pl.pallas_call(
        functools.partial(spread_kernel, sizes),
        out_shape=(shape, shape),
        in_specs=[anywhere] * 2,
        out_specs=(anywhere, anywhere),
        scratch_shapes=[
            pltpu.SemaphoreType.DMA((2, n)),
            pltpu.SemaphoreType.DMA((2, n)),
        ],
        compiler_params=pltpu.CompilerParams(collective_id=0, has_side_effects=True),
        name="spread_fields",
    )(cour, diff)


def swap_slots(sizes, slots, strips, which):
    n = sizes["tile"]
    half, rows = slots.shape[0], slots.shape[1]
    anywhere = pl.BlockSpec(memory_space=pl.ANY)
    return pl.pallas_call(
        functools.partial(swap_kernel, sizes),
        out_shape=jax.ShapeDtypeStruct((n, rows, C), slots.dtype),
        in_specs=[anywhere, anywhere],
        out_specs=anywhere,
        scratch_shapes=[
            pltpu.VMEM(strips.shape, jnp.float32),
            pltpu.VMEM(slots.shape, jnp.float32),
            pltpu.SemaphoreType.DMA((2, 2)),
            pltpu.SemaphoreType.DMA((half,)),
            pltpu.SemaphoreType.DMA((half,)),
            pltpu.SemaphoreType.DMA((2, half)),
            pltpu.SemaphoreType.DMA((2, half)),
            pltpu.SemaphoreType.DMA,
        ],
        compiler_params=pltpu.CompilerParams(collective_id=1 + which, has_side_effects=True),
        name=f"swap_slots_{which}",
    )(slots, strips)


def rows_of(planes, faces):
    return -(-(3 * planes + faces) // 8) * 8


def groups_of(planes):
    return -(-planes // 16)


def lanes(rows):
    return lax.broadcasted_iota(jnp.int32, (rows, C), 1)


def pack_part(planes, chunk, q, at, first, strips, turned):
    lane_group = lanes(C) // 8
    packed = jnp.zeros((C, C), jnp.float32)
    for slot in range(chunk):
        plane = q[pl.ds((at + slot) * C, C), :]
        packed = jnp.where(lane_group == slot, pltpu.roll(plane, 8 * slot + 3, 1), packed)
    turned[0:C, :] = packed.T
    for d in range(3):
        rows = pl.ds(first + d * planes, chunk)
        strips[0, rows, :] = turned[pl.ds(3 + d, chunk, stride=8), :]
        strips[1, rows, :] = turned[pl.ds(2 - d, chunk, stride=8), :]
        strips[2, rows, :] = q[pl.ds(at * C + d, chunk, stride=C), :]
        strips[3, rows, :] = q[pl.ds(at * C + C - 1 - d, chunk, stride=C), :]


def fill_slots(near, here, strips, slots):
    rows = slots.shape[1]
    for e in range(4):
        owner = near[0, e].astype(jnp.float32)
        strips[e, pl.ds(rows, 8), :] = jnp.full((8, C), owner, jnp.float32)

    @pl.loop(0, slots.shape[0])
    def _(i):
        dest = here[1] + i
        edge = jnp.int32(0)
        for e in range(1, 4):
            edge = jnp.where(near[0, e] == dest, e, edge)
        slots[i] = strips[edge, pl.ds(0, rows), :]


def pack_kernel(
    sizes, planes, roots, near, here, q, own_c, own_d, got_c0, got_c1, got_d0, got_d1,
    slots, strips, fields, turned
):
    chunk = chunk_of(planes)
    for part in range(planes // chunk):
        pack_part(planes, chunk, q, part * chunk, part * chunk, strips, turned)
    lane = lanes(C)
    faces = jnp.zeros((C, C), jnp.float32)
    for k, got in enumerate([(got_c0, got_d0), (got_c1, got_d1)]):
        mine = roots[k, 0] == here[0]
        for t, own in enumerate((own_c, own_d)):
            for lev in range(2):
                j = (k * 2 + t) * 2 + lev
                west = jnp.where(mine, own[0, k, 0, lev], got[t][0, 0, 0, lev])
                low = jnp.where(mine, own[0, k, 1, lev], got[t][0, 0, 1, lev])
                fields[k, t, 0, lev] = west
                fields[k, t, 1, lev] = low
                west = pltpu.roll(west, j, 1) if j else west
                faces = jnp.where(lane == j, west, faces)
                strips[2, pl.ds(3 * planes + j, 1), :] = low[0:1, :]
    strips[0, pl.ds(3 * planes, 8), :] = faces.T[0:8]
    strips[1, pl.ds(3 * planes, 8), :] = jnp.zeros((8, C), jnp.float32)
    strips[3, pl.ds(3 * planes, 8), :] = jnp.zeros((8, C), jnp.float32)
    fill_slots(near, here, strips, slots)


def field_spec(k):
    return pl.BlockSpec(
        (1, 1, 2, 2, C, C), lambda i, roots, *_: (roots[k, 0], k, 0, 0, 0, 0)
    )


def whole_spec(shape):
    return pl.BlockSpec(shape, lambda i, *_: (0,) * len(shape))


def pack_first(sizes, roots, near, here, q, cour, diff, cour_all, diff_all):
    planes = q.shape[0] // C
    half = sizes["tile"] // 2
    rows = rows_of(planes, 8)
    return pl.pallas_call(
        functools.partial(pack_kernel, sizes, planes),
        out_shape=(
            jax.ShapeDtypeStruct((half, rows, C), jnp.float32),
            jax.ShapeDtypeStruct((4, rows + 8, C), jnp.float32),
            jax.ShapeDtypeStruct((2, 2, 2, 2, C, C), jnp.float32),
        ),
        grid_spec=pltpu.PrefetchScalarGridSpec(
            num_scalar_prefetch=3,
            grid=(1,),
            in_specs=[
                whole_spec(q.shape),
                whole_spec(cour.shape),
                whole_spec(diff.shape),
                field_spec(0),
                field_spec(1),
                field_spec(0),
                field_spec(1),
            ],
            out_specs=(
                whole_spec((half, rows, C)),
                whole_spec((4, rows + 8, C)),
                whole_spec((2, 2, 2, 2, C, C)),
            ),
            scratch_shapes=[
                pltpu.VMEM((groups_of(planes) * C, C), jnp.float32),
            ],
        ),
        compiler_params=pltpu.CompilerParams(vmem_limit_bytes=VMEM_LIMIT),
        name="pack_first",
    )(
        roots,
        near,
        here,
        q,
        cour,
        diff,
        cour_all,
        cour_all,
        diff_all,
        diff_all,
    )


def orientation(flipped):
    row = lax.broadcasted_iota(jnp.int32, (C, C), 0)
    col = lax.broadcasted_iota(jnp.int32, (C, C), 1)
    target = jnp.where(flipped == 1, C - 1 - row, row)
    return jnp.where(col == target, 1.0, 0.0).astype(jnp.float32)


def oriented(rows, turn):
    return jnp.dot(
        rows, turn, precision=lax.Precision.HIGHEST, preferred_element_type=jnp.float32
    )


def taps(c, k):
    s = jnp.abs(c)
    rest = 1.0 - s
    mid = c * rest * rest
    outer = -s * rest
    ahead = (3.0 - 2.0 * s) * s
    pos = jnp.maximum(c, 0.0)
    neg = jnp.minimum(c, 0.0)
    out_pos = pos * outer
    out_neg = neg * outer
    a = 7.0 / 12.0
    b = -1.0 / 12.0
    return [
        b * out_pos,
        b * mid + a * out_pos,
        a * (mid + out_pos) + b * out_neg + pos * ahead + k,
        a * (mid + out_neg) + b * out_pos + neg * ahead - k,
        b * mid + a * out_neg,
        b * out_neg,
    ]


def stencil(low, high):
    zero = [None]
    lo = low + zero
    hi = zero + high
    result = []
    for a, b in zip(lo, hi):
        result.append(-b if a is None else a if b is None else a - b)
    return result


def chunk_of(planes):
    return math.gcd(planes, 16)


SHIFTS = (-3, -2, -1, 1, 2, 3)


def shift_weights(weights):
    row = lax.broadcasted_iota(jnp.int32, (3 * C, C), 0)
    col = lax.broadcasted_iota(jnp.int32, (3 * C, C), 1)
    item = row & 7
    outside = jnp.where(item < 3, item - 3, C - 3 + item)
    outside = jnp.where((row < 2 * C + 16) & (item < 6), outside, -C)
    source = jnp.where(row < 2 * C, row & (C - 1), outside)
    for i, shift in enumerate(SHIFTS):
        weights[:, i * C : (i + 1) * C] = jnp.where(source == col + shift, 1.0, 0.0).astype(
            jnp.bfloat16
        )


def halves(x):
    big = x.astype(jnp.bfloat16)
    return big, (x - big.astype(jnp.float32)).astype(jnp.bfloat16)


def step_kernel(sizes, planes, k, last, near, flips, here, q, fields, got_faces, got, *rest):
    if last:
        out, padded, turned, coef, south, faces, split, weights, moved = rest
    else:
        out, slots, strips, padded, turned, coef, south, faces, split, weights, moved = rest
    groups = groups_of(planes)
    chunk = chunk_of(planes)
    part = pl.program_id(0)

    @pl.loop(0, chunk)
    def _(i):
        p = part * chunk + i
        at = pl.multiple_of(p * C, C)
        plane = q[pl.ds(pl.multiple_of(i * C, C), C), :]
        padded[pl.ds(pl.multiple_of(p * PAD + 8, 8), C), :] = plane
        big, small = halves(plane)
        split[pl.ds(at, C), 0:C] = big
        split[pl.ds(at, C), C : 2 * C] = small

    @pl.when(part == 0)
    def _():
        shift_weights(weights)
        turned[...] = jnp.zeros_like(turned)
        for e in range(4):
            turn = orientation(flips[0, e])
            ghost = oriented(got[near[0, e]], turn)
            for d in range(3):
                part = ghost[d * planes : (d + 1) * planes]
                if e == 0:
                    turned[pl.ds(2 - d, planes, stride=8), :] = part
                elif e == 1:
                    turned[pl.ds(3 + d, planes, stride=8), :] = part
                elif e == 2:
                    padded[pl.ds(7 - d, planes, stride=PAD), :] = part
                else:
                    padded[pl.ds(C + 8 + d, planes, stride=PAD), :] = part
            if e in (1, 3):
                face = oriented(got_faces[near[0, e], pl.ds(3 * planes, 8), :], turn)
                if e == 1:
                    faces[...] = jnp.zeros_like(faces)
                    faces[0:8, :] = face
                else:
                    for t in range(2):
                        for lev in range(2):
                            j = (k * 2 + t) * 2 + lev
                            base = (t * 2 + lev) * (C + 8)
                            south[pl.ds(base, C), :] = fields[0, t, 1, lev]
                            south[pl.ds(base + C, 8), :] = jnp.broadcast_to(face[j : j + 1], (8, C))
        faces[...] = faces[...].T

        row = lax.broadcasted_iota(jnp.int32, (2 * C, C), 0)
        col = lax.broadcasted_iota(jnp.int32, (2 * C, C), 1)
        source = (row & 7) + 8 * (row // C)
        ghosts = [
            jnp.concatenate(halves(turned[pl.ds(g * C, C), :].T), axis=1) for g in range(groups)
        ]
        for slot in range(min(16, planes)):
            place = jnp.where((((row & (C - 1)) >> 3) == slot) & (source == col), 1.0, 0.0)
            place = place.astype(jnp.bfloat16)
            for g in range(groups):
                p = 16 * g + slot
                if p < planes:
                    split[pl.ds(p * C, C), 2 * C : 3 * C] = jnp.dot(
                        ghosts[g], place, preferred_element_type=jnp.float32
                    ).astype(jnp.bfloat16)

        lane8 = lanes(8)

        @pl.loop(0, C // 8)
        def _(r):
            at = pl.multiple_of(r * 8, 8)
            east = faces[pl.ds(at, 8), :]
            for lev in range(2):
                low_x, high_x, low_y, high_y = [], [], [], []
                for t in range(2):
                    j = (k * 2 + t) * 2 + lev
                    west = fields[0, t, 0, lev, pl.ds(at, 8), :]
                    low_x.append(west)
                    high_x.append(
                        jnp.where(
                            lane8 == C - 1, pltpu.roll(east, C - 1 - j, 1), pltpu.roll(west, C - 1, 1)
                        )
                    )
                    base = (t * 2 + lev) * (C + 8)
                    low_y.append(south[pl.ds(base + at, 8), :])
                    high_y.append(south[pl.ds(base + at + 1, 8), :])
                along_x = stencil(taps(*low_x), taps(*high_x))
                along_y = stencil(taps(*low_y), taps(*high_y))
                centre = 1.0 + along_x[3] + along_y[3]
                every = [centre] + along_x[:3] + along_x[4:] + along_y[:3] + along_y[4:]
                for i, value in enumerate(every):
                    coef[lev * 13 + i, pl.ds(at, 8), :] = value

    rows = min(4, chunk) * C

    @pl.loop(0, chunk * C // rows)
    def _(b):
        at = pl.multiple_of(part * (chunk * C) + b * rows, C)
        moved[pl.ds(pl.multiple_of(b * rows, C), rows), :] = jnp.dot(
            split[pl.ds(at, rows), :], weights[...], preferred_element_type=jnp.float32
        )

    @pl.loop(0, C // 8)
    def _(r):
        at = pl.multiple_of(r * 8, 8)
        for lev in range(2):
            w = [coef[lev * 13 + i, pl.ds(at, 8), :] for i in range(13)]
            for s in range(chunk // 2):
                p = 2 * s + lev
                base = (part * chunk + p) * PAD + 8 + at
                block = pl.ds(pl.multiple_of(p * C + at, 8), 8)
                total = w[0] * padded[pl.ds(base, 8), :]
                for i, d in enumerate(SHIFTS):
                    total += w[1 + i] * moved[block, i * C : (i + 1) * C]
                    total += w[7 + i] * padded[pl.ds(base + d, 8), :]
                out[block, :] = total

    if not last:
        pack_part(planes, chunk, out, 0, part * chunk, strips, turned)

        @pl.when(part == planes // chunk - 1)
        def _():
            fill_slots(near, here, strips, slots)


def advance(sizes, k, last, near, flips, here, q, fields, got_faces, got):
    planes = q.shape[0] // C
    half = sizes["tile"] // 2
    rows = rows_of(planes, 0)
    out_shape = [jax.ShapeDtypeStruct(q.shape, q.dtype)]
    chunk = chunk_of(planes)
    moving = pl.BlockSpec((chunk * C, C), lambda i, *_: (i, 0))
    out_specs = [moving]
    groups = groups_of(planes)
    scratch = [
        pltpu.VMEM((planes * PAD, C), jnp.float32),
        pltpu.VMEM((groups * C, C), jnp.float32),
        pltpu.VMEM((26, C, C), jnp.float32),
        pltpu.VMEM((4 * (C + 8), C), jnp.float32),
        pltpu.VMEM((C, C), jnp.float32),
        pltpu.VMEM((planes * C, 3 * C), jnp.bfloat16),
        pltpu.VMEM((3 * C, 6 * C), jnp.bfloat16),
        pltpu.VMEM((chunk_of(planes) * C, 6 * C), jnp.float32),
    ]
    if not last:
        for shape in ((half, rows, C), (4, rows + 8, C)):
            out_shape.append(jax.ShapeDtypeStruct(shape, q.dtype))
            out_specs.append(whole_spec(shape))
    return pl.pallas_call(
        functools.partial(step_kernel, sizes, planes, k, last),
        out_shape=out_shape,
        grid_spec=pltpu.PrefetchScalarGridSpec(
            num_scalar_prefetch=3,
            grid=(planes // chunk,),
            in_specs=[
                moving,
                pl.BlockSpec((1, 2, 2, 2, C, C), lambda i, *_: (k, 0, 0, 0, 0, 0)),
                whole_spec(got_faces.shape),
                whole_spec(got.shape),
            ],
            out_specs=out_specs,
            scratch_shapes=scratch,
        ),
        compiler_params=pltpu.CompilerParams(vmem_limit_bytes=VMEM_LIMIT),
        name=f"advance_{k}",
    )(near, flips, here, q, fields, got_faces, got)


def body(sizes, tracers, courant, diffusivity, edge_blocks, edge_flips, roots):
    q = tracers.reshape(-1, C)
    cour_all, diff_all = spread_fields(sizes, courant, diffusivity)
    half = sizes["tile"] // 2
    here = jnp.stack([lax.axis_index("spec"), lax.axis_index("tile") // half * half])
    slots, strips, fields = pack_first(
        sizes, roots, edge_blocks, here, q, courant, diffusivity, cour_all, diff_all
    )
    first = swap_slots(sizes, slots, strips, 0)
    block = (edge_blocks, edge_flips, here)
    q, slots, strips = advance(sizes, 0, False, *block, q, fields, first, first)
    second = swap_slots(sizes, slots, strips, 1)
    (q,) = advance(sizes, 1, True, *block, q, fields, first, second)
    return q.reshape(tracers.shape)


def solution(mesh):
    placed = (
        P("spec", None, "tile", None),
        P("spec", None, None, None, "tile", None),
        P("spec", None, None, None, "tile", None),
        P("tile", None),
        P("tile", None),
        P(None, "tile"),
    )
    return jax.shard_map(
        functools.partial(body, dict(mesh.shape)),
        mesh=mesh,
        in_specs=placed,
        out_specs=P("spec", None, "tile", None),
        check_vma=False,
    )
```
